256 devices in a mesh: row: 8 (over x_hi, y), col: 32 (over z, x_lo, core).
Axes of the slice: x: 4 (x_hi: 2, x_lo: 2; x = x_hi * 2 + x_lo), y: 4, z: 8, core: 2. Of those that a mesh axis runs over, the one named last changes fastest.
Arguments:
- samples: float32 [1024, 64, 128], P(('row', 'col')), may hold values from -6 to 6
- omega: float32 [8, 32, 100, 128, 128], P('row', 'col'), may hold values from -0.12 to 2.12
- block_rows: int32 [8, 32, 100], P('row', 'col'), may hold values from -1 to 1023, as said below
- block_cols: int32 [8, 32, 100], P('row', 'col'), may hold values from -1 to 1023, as said below
Outputs:
- omega_next: float32 [8, 32, 100, 128, 128], P('row', 'col')
The draws below stay inside these ranges and needn't reach their ends.
Inputs may be any that keep to these rules, and one draw needn't show every extreme that they name: `block_rows`: slots 0 to 3 of the device at (a, b) hold the diagonal blocks I = J = (a * 32 + b) * 4 + k in order of k; the other slots hold distinct off-diagonal blocks whose block row lies in a * 1024 / 8 up to (a + 1) * 1024 / 8 - 1 and whose block column J has (J // 4) % 32 = b; live slots come first and -1 fills the rest; some device has all 100 slots live. `block_cols`: -1 exactly where block_rows is -1.
All inputs are finite; a program needn't handle non-finite values.
Results may differ from the reference program's by a relative error of at most 0.0003.
Values sent between devices are 32-bit elements; how exact they have to be, the bound alone decides.
A program may use at most 128 MiB of HBM per device.

```python
import jax
import jax.numpy as jnp
from jax import lax

BS = 128
N_SAMP = 64
OFF_MOST = 96
ITERS = 2
NB = 1024
BPS = 4
CAP = 100
N_ROW = 8
N_COL = 32


def pattern_lists(key):
    pattern_key = jax.random.fold_in(key, 7)
    first_key, second_key, top_key, pick_key = jax.random.split(pattern_key, 4)
    devices_all = N_ROW * N_COL
    group_rows = NB // N_ROW
    group_cols = NB // N_COL
    factor_one = jax.random.randint(first_key, (devices_all,), 1, OFF_MOST + 1)
    factor_two = jax.random.randint(second_key, (devices_all,), 1, OFF_MOST + 1)
    active_counts = (factor_one * factor_two + OFF_MOST - 1) // OFF_MOST
    busiest = jax.random.randint(top_key, (), 0, devices_all)
    active_counts = jnp.where(jnp.arange(devices_all) == busiest, OFF_MOST, active_counts)

    def one_device(device, active_count):
        row_group = device // N_COL
        col_group = device % N_COL
        shuffled = jax.random.permutation(jax.random.fold_in(pick_key, device), group_rows * group_cols)
        local_row = shuffled // group_cols
        local_col = shuffled % group_cols
        global_row = row_group * group_rows + local_row
        global_col = (local_col // BPS * N_COL + col_group) * BPS + local_col % BPS
        is_diag = (global_row == global_col).astype(jnp.int32)
        ranked = jnp.argsort(is_diag, stable=True)[:OFF_MOST]
        kept_mask = jnp.arange(OFF_MOST) < active_count
        off_rows = jnp.where(kept_mask, global_row[ranked], -1)
        off_cols = jnp.where(kept_mask, global_col[ranked], -1)
        diag_ids = (row_group * N_COL + col_group) * BPS + jnp.arange(BPS)
        return (jnp.concatenate([diag_ids, off_rows]), jnp.concatenate([diag_ids, off_cols]))
    row_table, col_table = jax.vmap(one_device)(jnp.arange(devices_all), active_counts)
    row_table = row_table.reshape(N_ROW, N_COL, CAP).astype(jnp.int32)
    col_table = col_table.reshape(N_ROW, N_COL, CAP).astype(jnp.int32)
    return (row_table, col_table)


def draw_block_rows(key, part):
    return pattern_lists(key)[0]


def draw_block_cols(key, part):
    return pattern_lists(key)[1]


def draw_omega(key, part):
    noise_key, gain_key = jax.random.split(jax.random.fold_in(key, 11))
    full_shape = (N_ROW, N_COL, CAP, BS, BS)
    noise_part = 0.03 * jax.random.truncated_normal(noise_key, -4.0, 4.0, full_shape, jnp.float32)
    gain_values = jax.random.uniform(gain_key, (N_ROW, N_COL, CAP, BS), jnp.float32, 1.0, 2.0)
    diag_slot = (jnp.arange(CAP) < BPS).astype(jnp.float32)
    identity = jnp.eye(BS, dtype=jnp.float32)
    return noise_part + diag_slot[:, None, None] * gain_values[..., None] * identity


def level_of(own_key, extent, cuts, smallest, high):
    level = 1.0
    for axis_at, shards_of in cuts:
        heights = jax.random.uniform(jax.random.fold_in(jax.random.fold_in(own_key, 6), axis_at), (shards_of,), jnp.float32, smallest / len(cuts), high / len(cuts))
        level = level * jnp.repeat(jnp.exp(heights), extent[axis_at] // shards_of).reshape((-1,) + (1,) * (len(extent) - 1 - axis_at))
    return level


def normal_values(key, dims, scale, most, pieces=(), kind=jnp.bfloat16):
    drawn = scale * jax.random.normal(key, dims, jnp.float32)
    if pieces:
        drawn = drawn * level_of(key, dims, pieces, -0.22, 0.18)
    return jnp.clip(drawn, -most, most).astype(kind)


def setup_inputs(seed: int = 0) -> dict:
    key_of = jax.random.split(jax.random.key(seed), 5)
    return {
        "samples": normal_values(key_of[0], (NB, N_SAMP, BS), 1.0, 6.0, ((0, 256),), jnp.float32),
        "omega": draw_omega(jax.random.fold_in(key_of[4], 71), 0),
        "block_rows": draw_block_rows(jax.random.fold_in(key_of[4], 71), 0),
        "block_cols": draw_block_cols(jax.random.fold_in(key_of[4], 71), 0),
    }


STEP = 0.5
PENALTY = 0.1

def gradient_blocks(left_totals, right_samples, left_samples, right_totals, sample_count):
    forward = jnp.einsum('snb,snk->sbk', left_totals, right_samples, precision=lax.Precision.HIGHEST)
    mirrored = jnp.einsum('snb,snk->sbk', left_samples, right_totals, precision=lax.Precision.HIGHEST)
    return (forward + mirrored) * (0.5 / sample_count)

def proximal(current, grad, active, on_diagonal):
    stepped = current - STEP * grad
    eye_mask = jnp.eye(current.shape[-1], dtype=bool)[None] & on_diagonal[:, None, None]
    shrunk = jnp.sign(stepped) * jnp.maximum(jnp.abs(stepped) - STEP * PENALTY, 0.0)
    lifted = 0.5 * (stepped + jnp.sqrt(stepped * stepped + 4.0 * STEP))
    updated = jnp.where(eye_mask, lifted, shrunk)
    return jnp.where(active[:, None, None], updated, 0.0)

def reference(samples, omega, block_rows, block_cols):
    total_blocks = samples.shape[0]
    sample_count = samples.shape[1]
    width = samples.shape[2]
    current = omega.reshape(-1, CAP, width, width)
    row_lists = block_rows.reshape(-1, CAP)
    col_lists = block_cols.reshape(-1, CAP)
    for iteration in range(ITERS):

        def accumulate(totals, item):
            blocks, row_ids, col_ids = item
            active = row_ids >= 0
            picked = samples[jnp.where(active, col_ids, 0)]
            products = jnp.einsum('snk,sbk->snb', picked, blocks, precision=lax.Precision.HIGHEST)
            target = jnp.where(active, row_ids, total_blocks)
            return (totals.at[target].add(products, mode='drop'), None)
        start_totals = jnp.zeros((total_blocks, sample_count, width), jnp.float32)
        totals, unused = lax.scan(accumulate, start_totals, (current, row_lists, col_lists))

        def update(carry, item):
            blocks, row_ids, col_ids = item
            active = row_ids >= 0
            safe_rows = jnp.where(active, row_ids, 0)
            safe_cols = jnp.where(active, col_ids, 0)
            grad = gradient_blocks(totals[safe_rows], samples[safe_cols], samples[safe_rows], totals[safe_cols], sample_count)
            return (carry, proximal(blocks, grad, active, active & (row_ids == col_ids)))
        unused_carry, current = lax.scan(update, 0, (current, row_lists, col_lists))
    return current.reshape(omega.shape)
```

```python
import functools

import jax
import jax.numpy as jnp
from jax import lax
from jax.experimental import pallas as pl
from jax.experimental.pallas import tpu as pltpu
from jax.sharding import PartitionSpec as P

ITERS = 2
STEP = 0.5
PENALTY = 0.1

MESH = pl.DeviceIdType.MESH
F32 = jnp.float32
BF16 = jnp.bfloat16

Z = 8
Y = 4
K = 4
N = 64
B = 128
CHUNK = 20


class Place:
    def __init__(self):
        self.a = lax.axis_index("row")
        self.b = lax.axis_index("col")
        b = self.b
        self.z, self.x, self.c = b // 4, (b // 2) % 2, b % 2
        self.h, self.y = self.a // Y, self.a % Y

    def at_z(self, d):
        return (self.z + d + Z) % Z

    def at_y(self, d):
        return (self.y + d + Y) % Y

    def up(self):
        return (self.a, self.at_z(1) * 4 + self.x * 2 + self.c)

    def down(self):
        return (self.a, self.at_z(-1) * 4 + self.x * 2 + self.c)

    def side(self):
        return (self.a, self.z * 4 + (1 - self.x) * 2 + self.c)

    def twin(self):
        return (self.a, self.z * 4 + self.x * 2 + (1 - self.c))

    def north(self):
        return (self.h * Y + self.at_y(1), self.b)

    def south(self):
        return (self.h * Y + self.at_y(-1), self.b)

    def far(self):
        return ((1 - self.h) * Y + self.y, self.b)

    def everyone(self):
        return (self.up(), self.down(), self.side(), self.twin(),
                self.north(), self.south(), self.far())


class Wire:
    def __init__(self, send, recv):
        self.send, self.recv = send, recv
        self.copies = []

    def __call__(self, src, dst, device):
        i = len(self.copies)
        copy = pltpu.make_async_remote_copy(
            src_ref=src, dst_ref=dst, send_sem=self.send.at[i], recv_sem=self.recv.at[i],
            device_id=device, device_id_type=MESH)
        copy.start()
        self.copies.append(copy)
        return copy

    def finish(self):
        for copy in self.copies:
            copy.wait_send()


def greet(me):
    barrier = pltpu.get_barrier_semaphore()
    others = me.everyone()
    for device in others:
        pl.semaphore_signal(barrier, inc=1, device_id=device, device_id_type=MESH)
    pl.semaphore_wait(barrier, len(others))


class Gather:
    def __init__(self, me, wire, full, group):
        self.me, self.wire, self.full, self.group = me, wire, full, group
        self.twins = []
        self.rings = {}
        self.sides = {}
        self.rows = {}

    def part(self, zz, xx, lo, hi):
        return self.full.at[zz, xx, self.me.c, pl.ds(lo, hi - lo)]

    def to_twin(self, zz, xx, lo, hi, src=None):
        ref = self.part(zz, xx, lo, hi)
        self.twins.append(self.wire(ref if src is None else src, ref, self.me.twin()))

    def ring(self, name, d, zz, xx, lo, hi, src=None):
        for way, device in ((1, self.me.up()), (-1, self.me.down())):
            if zz[way] is None:
                continue
            ref = self.part(zz[way], xx, lo, hi)
            self.rings[name, way, d] = self.wire(ref if src is None else src, ref, device)

    def late(self, src=None):
        me = self.me
        ref = self.part(me.z, me.x, 2, 4)
        src = ref if src is None else src
        self.sides["late"] = self.wire(src, ref, me.side())
        self.ring("late", 1, {1: me.z, -1: me.z}, me.x, 2, 4, src)
        self.to_twin(me.z, me.x, 2, 4, src)

    def early(self, src=None):
        me = self.me
        ref = self.part(me.z, me.x, 0, 2)
        src = ref if src is None else src
        self.ring("early", 1, {1: me.z, -1: me.z}, me.x, 0, 2, src)
        self.sides["early", 0] = self.wire(src, ref, me.side())
        self.to_twin(me.z, me.x, 0, 2, src)

    def cross(self):
        me = self.me
        self.sides["late"].wait_recv()
        self.ring("cross", 1, {1: me.z, -1: me.z}, 1 - me.x, 2, 4)
        self.to_twin(me.z, 1 - me.x, 2, 4)

    def onward(self, name, d):
        me = self.me
        xx = 1 - me.x if name == "cross" else me.x
        lo, hi = (0, 2) if name == "early" else (2, 4)
        if d < 4:
            for way in (1, -1):
                self.rings[name, way, d].wait_recv()
                zz = me.at_z(-way * d)
                if d < 3:
                    self.ring(name, d + 1, {way: zz, -way: None}, xx, lo, hi)
                else:
                    mid = lo if way == 1 else lo + 1
                    self.ring(name, 4, {way: zz, -way: None}, xx, mid, mid + 1)
                if name == "early":
                    ref = self.part(zz, xx, lo, hi)
                    self.sides["early", way * d] = self.wire(ref, ref, me.side())
                self.to_twin(zz, xx, lo, hi)
        else:
            for way in (1, -1):
                self.rings[name, way, 4].wait_recv()
            zz = me.at_z(4)
            if name == "early":
                ref = self.part(zz, xx, lo, hi)
                self.sides["early", 4] = self.wire(ref, ref, me.side())
            self.to_twin(zz, xx, lo, hi)

    def sideways(self, d):
        me = self.me
        self.sides["early", d].wait_recv()
        self.to_twin(me.at_z(-d), 1 - me.x, 0, 2)

    def row_start(self, src):
        me = self.me
        ref = self.group.at[me.a]
        self.rows["far"] = self.wire(src, ref, me.far())
        self.rows[0, 1] = self.wire(src, ref, me.north())
        self.rows[0, -1] = self.wire(src, ref, me.south())

    def row_far(self):
        me = self.me
        self.rows["far"].wait_recv()
        ref = self.group.at[(1 - me.h) * Y + me.y]
        self.rows[1, 1] = self.wire(ref, ref, me.north())
        self.rows[1, -1] = self.wire(ref, ref, me.south())

    def row_onward(self, far):
        me = self.me
        hh = 1 - me.h if far else me.h
        for way, device, lo in ((1, me.north(), 0), (-1, me.south(), 2)):
            self.rows[far, way].wait_recv()
            ref = self.group.at[hh * Y + me.at_y(-way), pl.ds(lo, 2)]
            self.rows[far, way, "half"] = self.wire(ref, ref, device)

    def row_end(self):
        for far in (0, 1):
            for way in (1, -1):
                self.rows[far, way, "half"].wait_recv()

    def end(self):
        for copy in self.twins:
            copy.wait_recv()


def gather_rest(gather):
    gather.onward("late", 1)
    gather.cross()
    gather.onward("early", 1)
    gather.row_onward(0)
    gather.row_far()
    gather.sideways(0)
    gather.onward("late", 2)
    gather.onward("cross", 1)
    gather.onward("early", 2)
    gather.sideways(1)
    gather.sideways(-1)
    gather.onward("late", 3)
    gather.row_onward(1)
    gather.onward("cross", 2)
    gather.onward("early", 3)
    gather.sideways(2)
    gather.sideways(-2)
    gather.onward("late", 4)
    gather.onward("cross", 3)
    gather.onward("early", 4)
    gather.sideways(3)
    gather.sideways(-3)
    gather.onward("cross", 4)
    gather.sideways(4)
    gather.row_end()
    gather.end()


def gather_kernel(own, full, group, send, recv):
    me = Place()
    wire = Wire(send, recv)
    greet(me)
    gather = Gather(me, wire, full, group)
    gather.late(own.at[pl.ds(2, 2)])
    gather.early(own.at[pl.ds(0, 2)])
    gather.row_start(own)
    full[me.z, me.x, me.c] = own[...]
    group[me.a] = own[...]
    gather_rest(gather)
    wire.finish()


ORDER = (4, 3, -3, 2, -2, 1, -1, 0)


def reduce_kernel(part, full, group, total, ring, cross, last, send, recv):
    me = Place()
    wire = Wire(send, recv)
    greet(me)
    twin, side, hop = {}, {}, {}
    for d in ORDER:
        zz = me.at_z(d)
        twin[d] = wire(part.at[zz, :, 1 - me.c], total.at[zz], me.twin())

    def merge(d):
        zz = me.at_z(d)
        twin[d].wait_recv()
        total[zz] = total[zz] + part[zz, :, me.c]
        side[d] = wire(total.at[zz, 1 - me.x, pl.ds(2, 2)], cross.at[zz], me.side())

    def crossed(d):
        zz = me.at_z(d)
        side[d].wait_recv()
        total[zz, me.x, 2:4] = total[zz, me.x, 2:4] + cross[zz]

    def column(s):
        return (me.x, 0) if s == 0 else (1 - me.x, 0) if s == 1 else (me.x, 2)

    ways = ((0, 1, me.up()), (1, -1, me.down()))

    def first(s):
        xx, lo = column(s)
        for w, way, device in ways:
            hop[s, w, 0] = wire(total.at[me.at_z(4), xx, pl.ds(lo + w, 1)],
                                ring.at[s, w, 0, pl.ds(w, 1)], device)

    def onward(s, t):
        xx, lo = column(s)
        for w, way, device in ways:
            zz = me.at_z(way * (4 - t))
            hop[s, w, t - 1].wait_recv()
            if t == 1:
                ring[s, w, 0, w] = ring[s, w, 0, w] + total[zz, xx, lo + w]
                ring[s, w, 0, 1 - w] = total[zz, xx, lo + 1 - w]
            else:
                ring[s, w, t - 1] = ring[s, w, t - 1] + total[zz, xx, lo:lo + 2]
            hop[s, w, t] = wire(ring.at[s, w, t - 1], ring.at[s, w, t], device)

    def arrived(s):
        xx, lo = column(s)
        hop[s, 0, 3].wait_recv()
        hop[s, 1, 3].wait_recv()
        return total[me.z, xx, lo:lo + 2] + ring[s, 0, 3] + ring[s, 1, 3]

    merge(4)
    first(1)
    first(0)
    merge(3)
    merge(-3)
    crossed(4)
    first(2)
    merge(2)
    merge(-2)
    onward(1, 1)
    onward(0, 1)
    merge(1)
    merge(-1)
    merge(0)
    crossed(3)
    crossed(-3)
    onward(2, 1)
    onward(1, 2)
    onward(0, 2)
    crossed(2)
    crossed(-2)
    onward(2, 2)
    onward(1, 3)
    onward(0, 3)
    crossed(1)
    crossed(-1)
    onward(2, 3)
    ring[1, 0, 3] = arrived(1)
    swap = wire(ring.at[1, 0, 3], last, me.side())
    crossed(0)
    mine = full.at[me.z, me.x, me.c]
    mine[2:4] = arrived(2)
    gather = Gather(me, wire, full, group)
    gather.late()
    first_half = arrived(0)
    swap.wait_recv()
    mine[0:2] = first_half + last[...]
    gather.early()
    group[me.a] = mine[...]
    gather.row_start(mine)
    gather_rest(gather)
    wire.finish()


COPIES = 128


def gather_call(own):
    return pl.pallas_call(
        gather_kernel,
        name="gather_samples",
        out_shape=(jax.ShapeDtypeStruct((Z, 2, 2, K, N, B), F32),
                   jax.ShapeDtypeStruct((2 * Y, K, N, B), F32)),
        in_specs=[pl.BlockSpec(memory_space=pltpu.VMEM)],
        out_specs=(pl.BlockSpec(memory_space=pltpu.VMEM), pl.BlockSpec(memory_space=pltpu.VMEM)),
        scratch_shapes=[pltpu.SemaphoreType.DMA((COPIES,)), pltpu.SemaphoreType.DMA((COPIES,))],
        compiler_params=pltpu.CompilerParams(collective_id=0, has_side_effects=True),
    )(own)


def reduce_call(part):
    return pl.pallas_call(
        reduce_kernel,
        name="reduce_totals",
        out_shape=(jax.ShapeDtypeStruct((Z, 2, 2, K, N, B), F32),
                   jax.ShapeDtypeStruct((2 * Y, K, N, B), F32)),
        in_specs=[pl.BlockSpec(memory_space=pltpu.VMEM)],
        out_specs=(pl.BlockSpec(memory_space=pltpu.VMEM), pl.BlockSpec(memory_space=pltpu.VMEM)),
        scratch_shapes=[
            pltpu.VMEM((Z, 2, K, N, B), F32),
            pltpu.VMEM((3, 2, 4, 2, N, B), F32),
            pltpu.VMEM((Z, 2, N, B), F32),
            pltpu.VMEM((2, N, B), F32),
            pltpu.SemaphoreType.DMA((COPIES,)),
            pltpu.SemaphoreType.DMA((COPIES,)),
        ],
        compiler_params=pltpu.CompilerParams(collective_id=1, has_side_effects=True),
    )(part)


def split(v):
    high = v.astype(BF16)
    low = (v - high.astype(F32)).astype(BF16)
    return high, low


def slot_ids(rows, cols, s, group_rows):
    row = rows[s]
    col = cols[s]
    live = row >= 0
    local_row = jnp.maximum(row - lax.axis_index("row") * group_rows, 0)
    local_col = jnp.where(live, col // 128 * K + col % K, 0)
    return live, local_row, local_col


def product(picked, block):
    picked_high, picked_low = picked
    block_high, block_low = split(block)
    left = jnp.concatenate([picked_high, picked_high, picked_low], axis=1)
    right = jnp.concatenate([block_high, block_low, block_high], axis=1)
    return lax.dot_general(left, right, (((1,), (1,)), ((), ())), preferred_element_type=F32)


def gradient(row_total, row_sample, col_sample, col_total):
    (wi_h, wi_l), (xi_h, xi_l) = split(row_total), split(row_sample)
    (xj_h, xj_l), (wj_h, wj_l) = col_sample, split(col_total)
    left = jnp.concatenate([wi_h, xi_h, wi_h, xi_h, wi_l, xi_l], axis=0)
    right = jnp.concatenate([xj_h, wj_h, xj_l, wj_l, xj_h, wj_h], axis=0)
    return lax.dot_general(left, right, (((0,), (0,)), ((), ())), preferred_element_type=F32)


def first_kernel(rows, cols, omega, col_samples, partial):
    base = pl.program_id(0) * CHUNK
    group_rows = partial.shape[0]

    @pl.when(pl.program_id(0) == 0)
    def _():
        partial[...] = jnp.zeros_like(partial)

    def one(i, carry):
        live, r, j = slot_ids(rows, cols, base + i, group_rows)
        terms = product(split(col_samples[j]), omega[i])
        partial[r] = partial[r] + terms * jnp.where(live, 1.0, 0.0)
        return carry

    lax.fori_loop(0, CHUNK, one, 0, unroll=4)


def step_kernel(rows, cols, omega, row_samples, col_samples, row_totals, col_totals, out, partial=None):
    base = pl.program_id(0) * CHUNK
    group_rows = row_samples.shape[0]
    scale = STEP * 0.5 / N

    if partial is not None:
        @pl.when(pl.program_id(0) == 0)
        def _():
            partial[...] = jnp.zeros_like(partial)

    def one(i, carry, diagonal=False):
        live, r, j = slot_ids(rows, cols, base + i, group_rows)
        picked = split(col_samples[j])
        grad = gradient(row_totals[r], row_samples[r], picked, col_totals[j])
        stepped = omega[i] - scale * grad
        limit = jnp.where(live, STEP * PENALTY, 3e38)
        new = stepped - jnp.clip(stepped, -limit, limit)
        if diagonal:
            lifted = 0.5 * (stepped + jnp.sqrt(stepped * stepped + 4.0 * STEP))
            eye = (lax.broadcasted_iota(jnp.int32, (B, B), 0)
                   == lax.broadcasted_iota(jnp.int32, (B, B), 1))
            new = jnp.where(eye, lifted, new)
        out[i] = new
        if partial is not None:
            partial[r] = partial[r] + product(picked, new)
        return carry

    @pl.when(pl.program_id(0) == 0)
    def _():
        lax.fori_loop(0, K, functools.partial(one, diagonal=True), 0, unroll=2)
        lax.fori_loop(K, CHUNK, one, 0, unroll=4)

    @pl.when(pl.program_id(0) > 0)
    def _():
        lax.fori_loop(0, CHUNK, one, 0, unroll=4)


def whole(shape):
    return pl.BlockSpec(shape, lambda g, rows, cols: (0,) * len(shape), pipeline_mode=pl.Buffered(1))


def chunked():
    return pl.BlockSpec((CHUNK, B, B), lambda g, rows, cols: (g, 0, 0))


def kept(shape):
    return pl.BlockSpec(shape, lambda g, rows, cols: (0,) * len(shape))


def first_call(rows, cols, omega, col_samples, group_rows):
    return pl.pallas_call(
        first_kernel,
        name="first_terms",
        grid_spec=pltpu.PrefetchScalarGridSpec(
            num_scalar_prefetch=2,
            grid=(omega.shape[0] // CHUNK,),
            in_specs=[chunked(), whole(col_samples.shape)],
            out_specs=kept((group_rows, N, B)),
        ),
        out_shape=jax.ShapeDtypeStruct((group_rows, N, B), F32),
    )(rows, cols, omega, col_samples)


def step_call(rows, cols, omega, row_samples, col_samples, row_totals, col_totals, last):
    outs = [jax.ShapeDtypeStruct(omega.shape, F32)]
    out_specs = [chunked()]
    if not last:
        outs.append(jax.ShapeDtypeStruct(row_samples.shape, F32))
        out_specs.append(kept(row_samples.shape))
    return pl.pallas_call(
        step_kernel,
        name="last_step" if last else "step",
        grid_spec=pltpu.PrefetchScalarGridSpec(
            num_scalar_prefetch=2,
            grid=(omega.shape[0] // CHUNK,),
            in_specs=[chunked()] + [whole(v.shape) for v in (row_samples, col_samples, row_totals, col_totals)],
            out_specs=out_specs,
        ),
        out_shape=outs,
    )(rows, cols, omega, row_samples, col_samples, row_totals, col_totals)


def shards(samples, omega, block_rows, block_cols):
    current = omega[0, 0]
    rows = block_rows.reshape(-1)
    cols = block_cols.reshape(-1)
    full, group = gather_call(samples)
    row_samples = full.reshape(-1, N, B)
    col_samples = group.reshape(-1, N, B)
    partial = first_call(rows, cols, current, col_samples, row_samples.shape[0])
    for iteration in range(ITERS):
        full, group = reduce_call(partial.reshape(Z, 2, 2, K, N, B))
        row_totals = full.reshape(-1, N, B)
        col_totals = group.reshape(-1, N, B)
        outs = step_call(rows, cols, current, row_samples, col_samples, row_totals, col_totals,
                         iteration == ITERS - 1)
        current = outs[0]
        if iteration < ITERS - 1:
            partial = outs[1]
    return current[None, None]


def solution(mesh):
    return jax.shard_map(
        shards,
        mesh=mesh,
        in_specs=(
            P(("row", "col"), None, None),
            P("row", "col", None, None, None),
            P("row", "col", None),
            P("row", "col", None),
        ),
        out_specs=P("row", "col", None, None, None),
        check_vma=False,
    )
```
